32 devices in a mesh: bulk: 8 (over z, x), contact: 4 (over y, core).
Axes of the slice: x: 2, y: 2, z: 4, core: 2. Of those that a mesh axis runs over, the one named last changes fastest.
Arguments:
- k_inv: float32 [65536, 2048], P(('bulk', 'contact'))
- mortar_slave: float32 [8192, 256], P(('bulk', 'contact')), may hold values from -0.375 to 0.375
- mortar_master: float32 [8192, 256], P(('bulk', 'contact')), may hold values from -0.375 to 0.375
- force: float32 [65536, 256], P(('bulk', 'contact')), may hold values from -6 to 6
- lam_glue: float32 [8192, 256], P(('bulk', 'contact')), may hold values from -6 to 6
- lam_contact: float32 [8192, 256], P(('bulk', 'contact')), may hold values from 0 to 1
- master_map: int32 [32], P(('bulk', 'contact')), may hold values from 0 to 3, as said below
- on_surface: int32 [32], P(('bulk', 'contact')), may hold values 0 or 1
- step_type: int32 [2, 256], replicated, may hold values from 0 to 2
- active: int32 [2, 8192, 256], P(None, ('bulk', 'contact')), may hold values 0 or 1
- expand_len: float32 [256], replicated, may hold values from 0.05 to 0.3
Outputs:
- glue_final: float32 [8192, 256], P(('bulk', 'contact'))
- contact_final: float32 [8192, 256], P(('bulk', 'contact'))
- grad_glue_final: float32 [8192, 256], P(('bulk', 'contact'))
- grad_contact_final: float32 [8192, 256], P(('bulk', 'contact'))
The draws below stay inside these ranges and needn't reach their ends.
Inputs may be any that keep to these rules, and one draw needn't show every extreme that they name: master_map never names the subdomain's own position in its group of 4.
All inputs are finite; a program needn't handle non-finite values. No bound on the sum of `on_surface` or of `active` on one device may be relied on, other than what follows from the above.
Results may differ from the reference program's by a relative error of at most 0.0003.
Values sent between devices are 32-bit elements; how exact they have to be, the bound alone decides.
A program may use at most 128 MiB of HBM per device.

```python
import math
import jax
import jax.numpy as jnp
from jax import lax

NS = 2048
FACE = 256
MORTAR = 256
LOADS = 256
ITERS = 2
GROUP = 4
SUB = 32


def draw_k_inv(key, part):

    def single(index):
        sub_key = jax.random.fold_in(key, index)
        mixing = jax.random.normal(jax.random.fold_in(sub_key, 1), (NS, NS), jnp.float32)
        diag_part = jax.random.uniform(jax.random.fold_in(sub_key, 2), (NS,), jnp.float32, 0.5, 2.0)
        gram = jnp.dot(mixing, mixing.T, precision=lax.Precision.HIGHEST) / (2.0 * NS)
        result = gram + jnp.diag(diag_part)
        return result
    whole = lax.map(single, jnp.arange(SUB, dtype=jnp.int32))
    return whole.reshape(SUB * NS, NS)


def draw_master_map(key, part):
    offset = jax.random.randint(jax.random.fold_in(key, 7), (SUB,), 1, GROUP)
    offset = offset.at[0].set(GROUP - 1).at[1].set(GROUP - 1)
    position = jnp.arange(SUB, dtype=jnp.int32) % GROUP
    return ((position + offset) % GROUP).astype(jnp.int32)


def set_ends(values, stream_key, smallest, top_value):
    extent = values.shape
    index_at = [jax.random.randint(jax.random.fold_in(stream_key, axis), (), 0, extent[axis]) for axis in range(len(extent))]
    values = values.at[tuple(index_at)].set(smallest)
    longest = extent.index(max(extent))
    index_at[longest] = (index_at[longest] + 1) % extent[longest]
    return values.at[tuple(index_at)].set(top_value)


def steps_of(key, dims, pieces, least, largest):
    level = 1.0
    for dim, shards_of in pieces:
        draws = jax.random.uniform(jax.random.fold_in(jax.random.fold_in(key, 6), dim), (shards_of,), jnp.float32, least / len(pieces), largest / len(pieces))
        level = level * jnp.repeat(jnp.exp(draws), dims[dim] // shards_of).reshape((-1,) + (1,) * (len(dims) - 1 - dim))
    return level


def centred(own_key, dims, deviation, limit, pieces=(), held_as=jnp.bfloat16):
    array = jax.random.normal(own_key, dims, jnp.float32) * deviation
    if len(pieces) > 0:
        array = steps_of(own_key, dims, pieces, -0.22, 0.18) * array
    return jnp.clip(array, min=-limit, max=limit).astype(held_as)


def setup_inputs(seed: int = 0) -> dict:
    streams_of = jax.random.split(jax.random.key(seed), 12)
    k_inv = draw_k_inv(jax.random.fold_in(streams_of[11], 71), 0)
    mortar_slave = centred(streams_of[1], (SUB * MORTAR, MORTAR), MORTAR ** -0.5, 0.375, ((0, 32),), jnp.float32)
    mortar_master = centred(streams_of[2], (SUB * MORTAR, MORTAR), MORTAR ** -0.5, 0.375, ((0, 32),), jnp.float32)
    force = centred(streams_of[3], (SUB * NS, LOADS), 1.0, 6.0, ((0, 32),), jnp.float32)
    lam_glue = centred(streams_of[4], (SUB * FACE, LOADS), 1.0, 6.0, ((0, 32),), jnp.float32)
    lam_contact = jnp.clip(1.0 * jax.random.uniform(streams_of[5], (SUB * MORTAR, LOADS), jnp.float32) ** steps_of(streams_of[5], (SUB * MORTAR, LOADS), ((0, 32),), -0.2, 0.2), 0.0, 1.0)
    master_map = draw_master_map(jax.random.fold_in(streams_of[11], 71), 0)
    on_surface = set_ends((jax.random.randint(streams_of[7], (SUB,), 0, 2) < 1).astype(jnp.int32), jax.random.fold_in(streams_of[7], 1), 0, 1)
    step_type = set_ends(jax.random.randint(streams_of[8], (ITERS, LOADS), 0, 3), jax.random.fold_in(streams_of[8], 1), 0, 2).astype(jnp.int32)
    active = set_ends((jax.random.randint(streams_of[9], (ITERS, SUB * MORTAR, LOADS), 0, 4) < 1).astype(jnp.int32), jax.random.fold_in(streams_of[9], 1), 0, 1)
    expand_len = jnp.clip(jnp.exp(jax.random.uniform(streams_of[10], (LOADS,), jnp.float32, math.log(0.05), math.log(0.3))), 0.05, 0.3)
    return {"k_inv": k_inv, "mortar_slave": mortar_slave, "mortar_master": mortar_master, "force": force, "lam_glue": lam_glue, "lam_contact": lam_contact, "master_map": master_map, "on_surface": on_surface, "step_type": step_type, "active": active, "expand_len": expand_len}


precise = lax.Precision.HIGHEST


def inner(first_glue, first_contact, second_glue, second_contact):
    return jnp.sum(first_glue * second_glue, axis=(0, 1)) + jnp.sum(first_contact * second_contact, axis=(0, 1))


def reference(k_inv, mortar_slave, mortar_master, force, lam_glue, lam_contact, master_map, on_surface, step_type, active, expand_len):
    k_blocks = k_inv.reshape(SUB, NS, NS)
    slave_blocks = mortar_slave.reshape(SUB, MORTAR, MORTAR)
    master_blocks = mortar_master.reshape(SUB, MORTAR, MORTAR)
    load = force.reshape(SUB, NS, LOADS)
    surface = on_surface.astype(jnp.float32)[:, None, None]
    glue_mask = (jnp.arange(SUB) < SUB - GROUP).astype(jnp.float32)[:, None, None]
    master_pick = (master_map.reshape(SUB // GROUP, GROUP)[:, :, None] == jnp.arange(GROUP, dtype=jnp.int32)[None, None, :]).astype(jnp.float32)
    groups = SUB // GROUP

    def operate(glue_dual, contact_dual, primal_load):
        previous = jnp.concatenate([jnp.zeros((GROUP, FACE, LOADS), jnp.float32), glue_dual[:-GROUP]], axis=0)
        slave_term = jnp.einsum('smc,smr->scr', slave_blocks, contact_dual, precision=precise) * surface
        master_term = jnp.einsum('smc,smr->scr', master_blocks, contact_dual, precision=precise) * surface
        received = jnp.einsum('bjt,bjcr->btcr', master_pick, master_term.reshape(groups, GROUP, MORTAR, LOADS), precision=precise).reshape(SUB, MORTAR, LOADS)
        interior = jnp.zeros((SUB, NS - 2 * FACE - MORTAR, LOADS), jnp.float32)
        pushed = jnp.concatenate([-previous, glue_dual, slave_term - received, interior], axis=1) - primal_load
        response = jnp.einsum('sij,sjr->sir', k_blocks, pushed, precision=precise)
        following = jnp.concatenate([response[GROUP:, :FACE], jnp.zeros((GROUP, FACE, LOADS), jnp.float32)], axis=0)
        glue_out = (response[:, FACE:2 * FACE] - following) * glue_mask
        contact_face = response[:, 2 * FACE:2 * FACE + MORTAR]
        master_face = jnp.einsum('bjt,btcr->bjcr', master_pick, contact_face.reshape(groups, GROUP, MORTAR, LOADS), precision=precise).reshape(SUB, MORTAR, LOADS)
        own_gap = jnp.einsum('smc,scr->smr', slave_blocks, contact_face, precision=precise)
        other_gap = jnp.einsum('smc,scr->smr', master_blocks, master_face, precision=precise)
        return glue_out, (own_gap - other_gap) * surface

    glue_now = lam_glue.reshape(SUB, FACE, LOADS) * glue_mask
    contact_now = lam_contact.reshape(SUB, MORTAR, LOADS)
    grad_glue, grad_contact = operate(glue_now, contact_now, load)
    prev_glue = jnp.zeros_like(glue_now)
    prev_contact = jnp.zeros_like(contact_now)
    prev_image_glue = jnp.zeros_like(glue_now)
    prev_image_contact = jnp.zeros_like(contact_now)
    curvature = jnp.ones((LOADS,), jnp.float32)
    for sweep in range(ITERS):
        active_now = active[sweep].reshape(SUB, MORTAR, LOADS).astype(jnp.float32)
        kinds = step_type[sweep]
        is_cg = (kinds == 0).astype(jnp.float32)
        is_expand = (kinds == 1).astype(jnp.float32)
        is_chop = (kinds == 2).astype(jnp.float32)
        free_glue = grad_glue
        free_contact = grad_contact * (1.0 - active_now) * surface
        chopped = jnp.minimum(grad_contact, 0.0) * active_now * surface
        if sweep > 0:
            conj_ratio = inner(free_glue, free_contact, prev_image_glue, prev_image_contact) / curvature
        else:
            conj_ratio = jnp.zeros((LOADS,), jnp.float32)
        keep = is_cg + is_expand
        dir_glue = keep * free_glue - is_cg * conj_ratio * prev_glue
        dir_contact = keep * free_contact - is_cg * conj_ratio * prev_contact + is_chop * chopped
        image_glue, image_contact = operate(dir_glue, dir_contact, 0.0)
        descent = inner(grad_glue, grad_contact, dir_glue, dir_contact)
        curvature = inner(dir_glue, dir_contact, image_glue, image_contact)
        step_len = jnp.where(kinds == 1, expand_len, descent / curvature)
        half_glue = glue_now - step_len * dir_glue
        half_contact = contact_now - step_len * dir_contact
        correction = is_expand * surface * jnp.maximum(-half_contact, 0.0)
        fix_glue, fix_contact = operate(jnp.zeros_like(half_glue), correction, 0.0)
        glue_now = half_glue
        contact_now = half_contact + correction
        grad_glue = grad_glue - step_len * image_glue + fix_glue
        grad_contact = grad_contact - step_len * image_contact + fix_contact
        prev_glue, prev_contact = dir_glue, dir_contact
        prev_image_glue, prev_image_contact = image_glue, image_contact
    return (glue_now.reshape(SUB * FACE, LOADS), contact_now.reshape(SUB * MORTAR, LOADS),
            grad_glue.reshape(SUB * FACE, LOADS), grad_contact.reshape(SUB * MORTAR, LOADS))
```

```python
import functools

import jax
import jax.numpy as jnp
from jax import lax
from jax.experimental import pallas as pl
from jax.experimental.pallas import tpu as pltpu
from jax.sharding import PartitionSpec as P

MESH = pl.DeviceIdType.MESH
F32 = jnp.float32
BF16 = jnp.bfloat16


def split(x):
    high = x.astype(BF16)
    return high, (x - high.astype(F32)).astype(BF16)


def bdot(a, b):
    return jnp.dot(a, b, preferred_element_type=F32)


def dot3(a_high, a_low, x):
    width = x.shape[1]
    high, low = split(x)
    both = bdot(a_high, jnp.concatenate([high, low], axis=1))
    return both[:, :width] + (both[:, width:] + bdot(a_low, high))


def kernel(
    n_bulk, n_group,
    master_ref, surface_ref, kinv_ref, ms_ref, mm_ref, force_ref, lamg_ref, lamc_ref, kinds_ref, active_ref, expand_ref,
    outg_ref, outc_ref, outgg_ref, outgc_ref,
    k_raw, k_hi, k_lo, f_raw, f_hi, f_lo, base, gap_hi, gap_lo, adj_hi, adj_lo,
    w_ref, wfix, y_ref, gp, gl, zg, zc, tsrc, tslots, cslots, dg, dc, gg, gc, imz_g, imz_c, meta_src, meta,
    r1, r2,
    load_sem, gp_send, gp_recv, gl_send, gl_recv, t_send, t_recv, c_send, c_recv, m_send, m_recv,
    r1_send, r1_recv, r2_send, r2_recv,
):
    face, columns = lamg_ref.shape
    mortar = lamc_ref.shape[0]
    rows = 2 * face + mortar
    half = columns // 2
    b = lax.axis_index("bulk")
    c = lax.axis_index("contact")
    pairs = n_group // 2
    q = lax.div(c, 2)
    r = lax.rem(c, 2)
    partner = 2 * q + 1 - r
    pending = []

    barrier = pltpu.get_barrier_semaphore()
    for k in range(1, n_group):
        pl.semaphore_signal(barrier, inc=1, device_id={"bulk": b, "contact": lax.rem(c + k, n_group)}, device_id_type=MESH)
    for k in range(1, n_bulk):
        pl.semaphore_signal(barrier, inc=1, device_id={"bulk": lax.rem(b + k, n_bulk), "contact": c}, device_id_type=MESH)
    load_k = pltpu.make_async_copy(kinv_ref.at[pl.ds(0, rows)], k_raw, load_sem.at[0])
    load_f = pltpu.make_async_copy(force_ref, f_raw, load_sem.at[1])
    load_k.start()
    load_f.start()

    slot_ids = [partner]
    for k in range(1, pairs):
        there = lax.rem(q - k + pairs, pairs)
        slot_ids += [2 * there + r, 2 * there + 1 - r]

    def remote(src, dst, send, recv, where):
        return pltpu.make_async_remote_copy(
            src_ref=src, dst_ref=dst, send_sem=send, recv_sem=recv, device_id=where, device_id_type=MESH
        )

    def begin(copy):
        copy.start()
        pending.append(copy)

    def gather_start(src, slots, send, recv):
        for k in range(1, pairs):
            begin(remote(src, slots.at[2 * k - 1], send.at[2 * k - 1], recv.at[2 * k - 1],
                         {"bulk": b, "contact": 2 * lax.rem(q + k, pairs) + r}))
        begin(remote(src, slots.at[0], send.at[0], recv.at[0], {"bulk": b, "contact": partner}))

    def gather_relay(slots, send, recv):
        for k in range(1, pairs):
            remote(slots.at[2 * k - 1], slots.at[2 * k - 1], send.at[2 * k - 1], recv.at[2 * k - 1],
                   {"bulk": b, "contact": partner}).wait_recv()
            begin(remote(slots.at[2 * k - 1], slots.at[2 * k], send.at[2 * k], recv.at[2 * k],
                         {"bulk": b, "contact": partner}))

    def gather_end(slots, send, recv):
        for i in [0] + [2 * k for k in range(1, pairs)]:
            remote(slots.at[i], slots.at[i], send.at[i], recv.at[i], {"bulk": b, "contact": partner}).wait_recv()

    right = {"bulk": lax.rem(b + 1, n_bulk), "contact": c}
    left = {"bulk": lax.rem(b + n_bulk - 1, n_bulk), "contact": c}
    has_right = b < n_bulk - 1
    has_left = b > 0
    late = []

    def push_glue(src, p, h):
        copy = remote(src, gp.at[p, h], gp_send.at[p, h], gp_recv.at[p, h], right)

        @pl.when(has_right)
        def _():
            copy.start()

        late.append((has_right, copy))

    def push_glue_end(p, h):
        @pl.when(has_left)
        def _():
            remote(gp.at[p, h], gp.at[p, h], gp_send.at[p, h], gp_recv.at[p, h], left).wait_recv()

    def pull_glue(src, p, h):
        copy = remote(src, gl.at[p, h], gl_send.at[p, h], gl_recv.at[p, h], left)

        @pl.when(has_left)
        def _():
            copy.start()

        late.append((has_left, copy))

    def pull_glue_end(p, h):
        @pl.when(has_right)
        def _():
            remote(gl.at[p, h], gl.at[p, h], gl_send.at[p, h], gl_recv.at[p, h], right).wait_recv()

    @pl.when(b == 0)
    def _():
        gp[...] = jnp.zeros_like(gp)

    @pl.when(b == n_bulk - 1)
    def _():
        gl[...] = jnp.zeros_like(gl)

    surface = surface_ref[0].astype(F32)
    own_master = jnp.full((8, half), master_ref[0].astype(F32), F32)
    meta_src[...] = own_master
    mask = jnp.where(has_right, 1.0, 0.0).astype(F32)
    slave = ms_ref[...] * surface
    master = mm_ref[...] * surface
    for i, part in enumerate((slave, -master)):
        high, low = split(part)
        gap_hi[:, i * mortar : (i + 1) * mortar] = high
        gap_lo[:, i * mortar : (i + 1) * mortar] = low
    for i, part in enumerate((slave, master)):
        high, low = split(part.T)
        adj_hi[i * mortar : (i + 1) * mortar, :] = high
        adj_lo[i * mortar : (i + 1) * mortar, :] = low

    def cols(h):
        return slice(h * half, (h + 1) * half)

    def send_mortar(dual, p, h):
        both = dot3(adj_hi[...], adj_lo[...], dual)
        tsrc[p, h] = both[mortar:]
        return both[:mortar]

    def mortar_start(p, h):
        gather_start(tsrc.at[p, h], tslots.at[p, h], t_send.at[p, h], t_recv.at[p, h])

    def mortar_end(p, h):
        gather_end(tslots.at[p, h], t_send.at[p, h], t_recv.at[p, h])
        total = 0.0
        for i in range(n_group - 1):
            total = total + jnp.where(meta[i, 0:1, :] == c.astype(F32), tslots[p, h, i], 0.0)
        return total

    def mortar_relay(p, h):
        gather_relay(tslots.at[p, h], t_send.at[p, h], t_recv.at[p, h])

    def face_start(p, h):
        gather_start(y_ref.at[p, h, pl.ds(2 * face, mortar)], cslots.at[p, h], c_send.at[p, h], c_recv.at[p, h])
        pull_glue(y_ref.at[p, h, pl.ds(0, face)], p, h)

    def face_relay(p, h):
        gather_relay(cslots.at[p, h], c_send.at[p, h], c_recv.at[p, h])

    def face_end(p, h):
        gather_end(cslots.at[p, h], c_send.at[p, h], c_recv.at[p, h])
        chosen = 0.0
        for i, ident in enumerate(slot_ids):
            chosen = chosen + jnp.where(own_master[0:1, :] == ident.astype(F32), cslots[p, h, i], 0.0)
        stacked = jnp.concatenate([y_ref[p, h, 2 * face :, :], chosen], axis=0)
        gap = dot3(gap_hi[...], gap_lo[...], stacked)
        pull_glue_end(p, h)
        return (y_ref[p, h, face : 2 * face, :] - gl[p, h]) * mask, gap

    def apply(w_value, p, h, first, plus):
        high, low = split(w_value)
        both = jnp.concatenate([high, low], axis=1)
        cut = pl.ds(first, w_value.shape[0])
        for i in range(3):
            at = pl.ds(i * face, face)
            out = bdot(k_hi[at, cut], both)
            out = out[:, :half] + (out[:, half:] + bdot(k_lo[at, cut], high))
            if plus:
                out = out + base[h, at, :]
            y_ref[p, h, at, :] = out

    def sums_start(n, h, values):
        padded = values + [jnp.zeros_like(values[0])] * (8 - len(values))
        r1[n, h, c] = jnp.concatenate(padded, axis=0)
        for k in range(1, n_group):
            begin(remote(r1.at[n, h, c], r1.at[n, h, c], r1_send.at[n, h, k], r1_recv.at[n, h, k],
                         {"bulk": b, "contact": lax.rem(c + k, n_group)}))

    def sums_mid(n, h):
        for k in range(1, n_group):
            there = lax.rem(c - k + n_group, n_group)
            remote(r1.at[n, h, there], r1.at[n, h, there], r1_send.at[n, h, k], r1_recv.at[n, h, k],
                   {"bulk": b, "contact": there}).wait_recv()
        r2[n, h, b] = jnp.sum(r1[n, h], axis=0)
        for k in range(1, n_bulk):
            begin(remote(r2.at[n, h, b], r2.at[n, h, b], r2_send.at[n, h, k], r2_recv.at[n, h, k],
                         {"bulk": lax.rem(b + k, n_bulk), "contact": c}))

    def sums_end(n, h):
        for k in range(1, n_bulk):
            there = lax.rem(b - k + n_bulk, n_bulk)
            remote(r2.at[n, h, there], r2.at[n, h, there], r2_send.at[n, h, k], r2_recv.at[n, h, k],
                   {"bulk": there, "contact": c}).wait_recv()
        return jnp.sum(r2[n, h], axis=0)

    def inner(*terms):
        return sum(jnp.sum(x * y, axis=0, keepdims=True) for x, y in terms)

    for h in range(2):
        w_ref[0, h, 2 * face :, :] = send_mortar(lamc_ref[:, cols(h)], 0, h)
    pl.semaphore_wait(barrier, n_group - 1 + n_bulk - 1)
    for i in range(n_group - 1):
        to = slot_ids[i]
        k = (i + 1) // 2
        mirror = i if i == 0 else 2 * (pairs - k) - (i % 2)
        begin(remote(meta_src, meta.at[mirror], m_send.at[i], m_recv.at[mirror], {"bulk": b, "contact": to}))
    for h in range(2):
        mortar_start(0, h)
        push_glue(lamg_ref.at[:, pl.ds(h * half, half)], 0, h)

    load_f.wait()
    high, low = split(-f_raw[...])
    f_hi[...] = high
    f_lo[...] = low
    load_k.wait()

    @pl.loop(0, 3)
    def _(i):
        at = pl.ds(pl.multiple_of(i * face, face), face)
        high, low = split(k_raw[at, :])
        k_hi[at, :] = high
        k_lo[at, :] = low
        out = bdot(k_hi[at, :], f_hi[...])
        out = out + (bdot(k_hi[at, :], f_lo[...]) + bdot(k_lo[at, :], f_hi[...]))
        for h in range(2):
            base[h, at, :] = out[:, h * half : (h + 1) * half]

    for i in range(n_group - 1):
        remote(meta.at[i], meta.at[i], m_send.at[i], m_recv.at[i], {"bulk": b, "contact": partner}).wait_recv()

    for h in range(2):
        mortar_relay(0, h)
        push_glue_end(0, h)
        own = w_ref[0, h, 2 * face :, :]
        w = jnp.concatenate([-gp[0, h], lamg_ref[:, cols(h)] * mask, own - mortar_end(0, h)], axis=0)
        apply(w, 0, h, 0, True)
        face_start(0, h)

    for h in range(2):
        face_relay(0, h)
        grad_g, grad_c = face_end(0, h)
        gg[h] = grad_g
        gc[h] = grad_c
        kind = kinds_ref[0:1, cols(h)]
        length = expand_ref[0:1, cols(h)]
        expand = kind == 1
        chop = kind == 2
        held = active_ref[0, :, cols(h)].astype(F32)
        dir_g = jnp.where(chop, 0.0, grad_g)
        dir_c = jnp.where(chop, jnp.minimum(grad_c, 0.0) * held, grad_c * (1.0 - held)) * surface
        scale = jnp.where(expand, length, 1.0)
        dg[h] = dir_g
        dc[h] = dir_c
        z_c = scale * dir_c
        fix = jnp.where(expand, surface * jnp.maximum(z_c - lamc_ref[:, cols(h)], 0.0), 0.0)
        zg[0, h] = scale * dir_g
        push_glue(zg.at[0, h], 1, h)
        zc[0, h] = z_c - fix
        w_ref[0, h, 2 * face :, :] = send_mortar(zc[0, h], 1, h)
        mortar_start(1, h)
        wfix[h] = send_mortar(fix, 2, h)
    for h in range(2):
        mortar_start(2, h)

    for h in range(2):
        mortar_relay(1, h)
        push_glue_end(1, h)
        own = w_ref[0, h, 2 * face :, :]
        w = jnp.concatenate([-gp[1, h], zg[0, h], own - mortar_end(1, h)], axis=0)
        w_ref[0, h] = w
        apply(w, 1, h, 0, False)
        face_start(1, h)
        sums_start(0, h, [
            inner((gg[h], dg[h]), (gc[h], dc[h])),
            inner((w, y_ref[1, h])),
        ])
    for h in range(2):
        mortar_relay(2, h)
        sums_mid(0, h)
    for h in range(2):
        w = wfix[h] - mortar_end(2, h)
        wfix[h] = w
        apply(w, 2, h, 2 * face, False)

    for h in range(2):
        face_relay(1, h)
        b_g, b_c = face_end(1, h)
        imz_g[h] = b_g
        imz_c[h] = b_c
        sums = sums_end(0, h)
        step = jnp.where(kinds_ref[0:1, cols(h)] == 1, 1.0, sums[0:1] / sums[1:2])
        grad_g = gg[h] - step * b_g
        grad_c = gc[h] - step * b_c
        lam_c = lamc_ref[:, cols(h)] - step * zc[0, h]
        outg_ref[:, cols(h)] = lamg_ref[:, cols(h)] * mask - step * zg[0, h]
        outc_ref[:, cols(h)] = lam_c
        gg[h] = grad_g
        gc[h] = grad_c
        kind = kinds_ref[1:2, cols(h)]
        expand = kind == 1
        chop = kind == 2
        held = active_ref[1, :, cols(h)].astype(F32)
        scale = jnp.where(expand, expand_ref[0:1, cols(h)], 1.0)
        zg[1, h] = jnp.where(chop, 0.0, scale * grad_g)
        push_glue(zg.at[1, h], 2, h)
        v_c = jnp.where(chop, jnp.minimum(grad_c, 0.0) * held, scale * (grad_c * (1.0 - held))) * surface
        zc[1, h] = v_c - jnp.where(expand, surface * jnp.maximum(v_c - lam_c, 0.0), 0.0)
        w_ref[1, h, 2 * face :, :] = send_mortar(zc[1, h], 3, h)
        mortar_start(3, h)
    for h in range(2):
        face_start(2, h)

    def scale_of(h):
        return jnp.where(kinds_ref[0:1, cols(h)] == 1, expand_ref[0:1, cols(h)], 1.0)

    for h in range(2):
        mortar_relay(3, h)
        push_glue_end(2, h)
        own = w_ref[1, h, 2 * face :, :]
        w = jnp.concatenate([-gp[2, h], zg[1, h], own - mortar_end(3, h)], axis=0)
        apply(w, 3, h, 0, False)
        face_start(3, h)
        w_0 = jnp.concatenate([w_ref[0, h, : 2 * face, :], w_ref[0, h, 2 * face :, :] + wfix[h]], axis=0)
        y_0 = y_ref[1, h] + y_ref[2, h]
        inverse = 1.0 / scale_of(h)
        y_v = y_ref[3, h]
        sums_start(1, h, [
            inner((w, y_0)) * inverse,
            inner((w, y_v)),
            inner((w_0, y_v)) * inverse,
            inner((gg[h], zg[1, h]), (gc[h], zc[1, h])),
            inner((gg[h], dg[h]), (gc[h], dc[h])),
            inner((w_0, y_0)) * inverse * inverse,
        ])
    for h in range(2):
        face_relay(2, h)
        sums_mid(1, h)

    for h in range(2):
        f_g, f_c = face_end(2, h)
        inverse = 1.0 / scale_of(h)
        imz_g[h] = (imz_g[h] + f_g) * inverse
        imz_c[h] = (imz_c[h] + f_c) * inverse
        face_relay(3, h)
    for h in range(2):
        b_g, b_c = face_end(3, h)
        sums = sums_end(1, h)
        kind = kinds_ref[1:2, cols(h)]
        gamma = jnp.where(kind == 0, sums[0:1] / sums[5:6], 0.0)
        curvature = sums[1:2] - gamma * (sums[2:3] + sums[0:1]) + gamma * gamma * sums[5:6]
        descent = sums[3:4] - gamma * sums[4:5]
        step = jnp.where(kind == 1, 1.0, descent / curvature)
        outg_ref[:, cols(h)] = outg_ref[:, cols(h)] - step * (zg[1, h] - gamma * dg[h])
        outc_ref[:, cols(h)] = outc_ref[:, cols(h)] - step * (zc[1, h] - gamma * dc[h])
        outgg_ref[:, cols(h)] = gg[h] - step * (b_g - gamma * imz_g[h])
        outgc_ref[:, cols(h)] = gc[h] - step * (b_c - gamma * imz_c[h])

    for copy in pending:
        copy.wait_send()
    for there, copy in late:
        @pl.when(there)
        def _(copy=copy):
            copy.wait_send()


def finish(a, b, c, d, oa, ob, oc, od, sem):
    copies = [pltpu.make_async_copy(x, y, sem.at[i]) for i, (x, y) in enumerate(((a, oa), (b, ob), (c, oc), (d, od)))]
    for copy in copies:
        copy.start()
    for copy in copies:
        copy.wait()


def settle(parts):
    shape = jax.ShapeDtypeStruct(parts[0].shape, F32)
    return tuple(pl.pallas_call(
        finish,
        out_shape=[shape] * 4,
        in_specs=[pl.BlockSpec(memory_space=pltpu.VMEM)] * 4,
        out_specs=[pl.BlockSpec(memory_space=pl.ANY)] * 4,
        scratch_shapes=[pltpu.SemaphoreType.DMA((4,))],
    )(*[pltpu.with_memory_space_constraint(x, pltpu.VMEM) for x in parts]))


def solution(mesh):
    n_bulk, n_group = mesh.shape["bulk"], mesh.shape["contact"]
    split_rows = P(("bulk", "contact"), None)
    ids = P(("bulk", "contact"))
    placed = (split_rows,) * 6 + (ids, ids, P(), P(None, ("bulk", "contact"), None), P())

    def per_device(k_inv, ms, mm, force, lam_g, lam_c, master_map, on_surface, kinds, active, expand_len):
        face, columns = lam_g.shape
        mortar = lam_c.shape[0]
        order = k_inv.shape[1]
        rows = 2 * face + mortar
        half = columns // 2
        slots = n_group - 1
        vmem = pltpu.VMEM
        dma = pltpu.SemaphoreType.DMA
        in_vmem = pl.BlockSpec(memory_space=vmem)
        in_smem = pl.BlockSpec(memory_space=pltpu.SMEM)
        anywhere = pl.BlockSpec(memory_space=pl.ANY)
        dual = lambda *lead: vmem(lead + (2, face, half), F32)
        return settle(pl.pallas_call(
            functools.partial(kernel, n_bulk, n_group),
            out_shape=[pltpu.VMEM((face, columns), F32)] * 4,
            in_specs=[in_smem, in_smem, anywhere, in_vmem, in_vmem, anywhere] + [in_vmem] * 5,
            out_specs=[in_vmem] * 4,
            scratch_shapes=[
                vmem((rows, order), F32), vmem((rows, order), BF16), vmem((rows, order), BF16),
                vmem((order, columns), F32), vmem((order, columns), BF16), vmem((order, columns), BF16),
                vmem((2, rows, half), F32),
                vmem((mortar, 2 * mortar), BF16), vmem((mortar, 2 * mortar), BF16),
                vmem((2 * mortar, mortar), BF16), vmem((2 * mortar, mortar), BF16),
                vmem((2, 2, rows, half), F32), dual(), vmem((4, 2, rows, half), F32),
                dual(3), dual(4), dual(2), dual(2), dual(4),
                vmem((4, 2, slots, mortar, half), F32), vmem((4, 2, slots, mortar, half), F32),
                dual(), dual(), dual(), dual(), dual(), dual(),
                vmem((8, half), F32), vmem((slots, 8, half), F32),
                vmem((2, 2, n_group, 8, half), F32), vmem((2, 2, n_bulk, 8, half), F32),
                dma((2,)), dma((3, 2)), dma((3, 2)), dma((4, 2)), dma((4, 2)),
                dma((4, 2, slots)), dma((4, 2, slots)), dma((4, 2, slots)), dma((4, 2, slots)),
                dma((slots,)), dma((slots,)),
                dma((2, 2, n_group)), dma((2, 2, n_group)), dma((2, 2, n_bulk)), dma((2, 2, n_bulk)),
            ],
            compiler_params=pltpu.CompilerParams(
                collective_id=0, has_side_effects=True, vmem_limit_bytes=60 * 1024 * 1024
            ),
        )(master_map, on_surface, k_inv, ms, mm, force, lam_g, lam_c, kinds, active, expand_len.reshape(1, -1)))

    return jax.shard_map(
        per_device, mesh=mesh, in_specs=placed, out_specs=(split_rows,) * 4, check_vma=False
    )
```

```python
import functools

import jax
import jax.numpy as jnp
from jax import lax
from jax.experimental import pallas as pl
from jax.experimental.pallas import tpu as pltpu
from jax.sharding import PartitionSpec as P

MESH = pl.DeviceIdType.MESH
F32 = jnp.float32
BF16 = jnp.bfloat16


def split(x):
    high = x.astype(BF16)
    return high, (x - high.astype(F32)).astype(BF16)


def bdot(a, b):
    return jnp.dot(a, b, preferred_element_type=F32)


def dot3(a_high, a_low, x):
    width = x.shape[1]
    high, low = split(x)
    both = bdot(a_high, jnp.concatenate([high, low], axis=1))
    return both[:, :width] + (both[:, width:] + bdot(a_low, high))


def kernel(
    n_bulk, n_group,
    master_hbm, surface_hbm, kinv_hbm, ms_hbm, mm_hbm, force_hbm, lamg_hbm, lamc_hbm, kinds_hbm, active_hbm, expand_hbm,
    outg_ref, outc_ref, outgg_ref, outgc_ref,
    master_ref, surface_ref, ms_ref, mm_ref, lamg_ref, lamc_ref, kinds_ref, active_ref, expand_ref,
    k_raw, k_hi, k_lo, f_raw, f_hi, f_lo, base, gap_hi, gap_lo, adj_hi, adj_lo,
    w_ref, wfix, y_ref, gp, gl, zg, zc, tsrc, tpart, tout, tin, cpart, cout, cin,
    dg, dc, gg, gc, imz_g, imz_c, own_gap, meta_src, meta, r1, r2,
    load_sem, k_sem, gp_send, gp_recv, gl_send, gl_recv, tp_send, tp_recv, tx_send, tx_recv,
    cp_send, cp_recv, cx_send, cx_recv, m_send, m_recv, r1_send, r1_recv, r2_send, r2_recv,
):
    face, columns = lamg_ref.shape
    mortar = lamc_ref.shape[0]
    rows = 2 * face + mortar
    half = columns // 2
    b = lax.axis_index("bulk")
    c = lax.axis_index("contact")
    pairs = n_group // 2
    q = lax.div(c, 2)
    r = lax.rem(c, 2)
    partner = 2 * q + 1 - r
    pending = []

    barrier = pltpu.get_barrier_semaphore()
    for k in range(1, n_group):
        pl.semaphore_signal(barrier, inc=1, device_id={"bulk": b, "contact": lax.rem(c + k, n_group)}, device_id_type=MESH)
    for k in range(1, n_bulk):
        pl.semaphore_signal(barrier, inc=1, device_id={"bulk": lax.rem(b + k, n_bulk), "contact": c}, device_id_type=MESH)

    def load(i, src, dst):
        copy = pltpu.make_async_copy(src, dst, load_sem.at[i])
        copy.start()
        return copy

    def k_load(i):
        at = pl.ds(pl.multiple_of(i * face, face), face)
        return pltpu.make_async_copy(kinv_hbm.at[at], k_raw.at[at], k_sem.at[i])

    load_mm = load(0, mm_hbm, mm_ref)
    load_lamc = load(1, lamc_hbm, lamc_ref)
    load_master = load(2, master_hbm, master_ref)
    load_surface = load(3, surface_hbm, surface_ref)
    load_lamg = load(4, lamg_hbm, lamg_ref)
    load_ms = load(5, ms_hbm, ms_ref)
    load_f = load(6, force_hbm, f_raw)
    for i in range(3):
        k_load(i).start()
    load_kinds = load(7, kinds_hbm, kinds_ref)
    load_expand = load(8, expand_hbm, expand_ref)
    load_active = load(9, active_hbm, active_ref)

    others = range(1, pairs)

    def other(k):
        return 2 * lax.rem(q + k, pairs) + r

    def remote(src, dst, send, recv, where):
        return pltpu.make_async_remote_copy(
            src_ref=src, dst_ref=dst, send_sem=send, recv_sem=recv, device_id=where, device_id_type=MESH
        )

    def begin(copy):
        copy.start()
        pending.append(copy)

    def near(where):
        return {"bulk": b, "contact": where}

    right = {"bulk": lax.rem(b + 1, n_bulk), "contact": c}
    left = {"bulk": lax.rem(b + n_bulk - 1, n_bulk), "contact": c}
    has_right = b < n_bulk - 1
    has_left = b > 0
    late = []

    def push_glue(src, p, h):
        copy = remote(src, gp.at[p, h], gp_send.at[p, h], gp_recv.at[p, h], right)

        @pl.when(has_right)
        def _():
            copy.start()

        late.append((has_right, copy))

    def push_glue_end(p, h):
        @pl.when(has_left)
        def _():
            remote(gp.at[p, h], gp.at[p, h], gp_send.at[p, h], gp_recv.at[p, h], left).wait_recv()

    def pull_glue(p, h):
        copy = remote(y_ref.at[p, h, pl.ds(0, face)], gl.at[p, h], gl_send.at[p, h], gl_recv.at[p, h], left)

        @pl.when(has_left)
        def _():
            copy.start()

        late.append((has_left, copy))

    def pull_glue_end(p, h):
        @pl.when(has_right)
        def _():
            remote(gl.at[p, h], gl.at[p, h], gl_send.at[p, h], gl_recv.at[p, h], right).wait_recv()

    def cols(h):
        return slice(h * half, (h + 1) * half)

    def pick(row, ident, value):
        return jnp.where(row == ident.astype(F32), value, 0.0)

    def adjoint(parts, first):
        high, low = parts
        cut = pl.ds(first, mortar)
        both = bdot(adj_hi[cut, :], jnp.concatenate([high, low], axis=1))
        return both[:, :half] + (both[:, half:] + bdot(adj_lo[cut, :], high))

    def mortar_swap(p, h):
        begin(remote(tsrc.at[p, h], tpart.at[p, h], tp_send.at[p, h], tp_recv.at[p, h], near(partner)))

    def mortar_cross(p, h):
        remote(tpart.at[p, h], tpart.at[p, h], tp_send.at[p, h], tp_recv.at[p, h], near(partner)).wait_recv()
        for k in others:
            to = other(k)
            tout[p, h, k - 1] = pick(own_row, to, tsrc[p, h]) + pick(meta[0, 0:1, :], to, tpart[p, h])
            begin(remote(tout.at[p, h, k - 1], tin.at[p, h, k - 1], tx_send.at[p, h, k - 1], tx_recv.at[p, h, k - 1], near(to)))

    def mortar_end(p, h):
        total = pick(meta[0, 0:1, :], c, tpart[p, h])
        for k in others:
            remote(tin.at[p, h, k - 1], tin.at[p, h, k - 1], tx_send.at[p, h, k - 1], tx_recv.at[p, h, k - 1],
                   near(other(k))).wait_recv()
            total = total + tin[p, h, k - 1]
        return total

    def face_swap(p, h):
        begin(remote(y_ref.at[p, h, pl.ds(2 * face, mortar)], cpart.at[p, h], cp_send.at[p, h], cp_recv.at[p, h], near(partner)))

    def face_cross(p, h):
        remote(cpart.at[p, h], cpart.at[p, h], cp_send.at[p, h], cp_recv.at[p, h], near(partner)).wait_recv()
        for k in others:
            row = meta[pairs - k, 0:1, :]
            cout[p, h, k - 1] = pick(row, c, y_ref[p, h, 2 * face :, :]) + pick(row, partner, cpart[p, h])
            begin(remote(cout.at[p, h, k - 1], cin.at[p, h, k - 1], cx_send.at[p, h, k - 1], cx_recv.at[p, h, k - 1],
                         near(other(k))))
        own_gap[p, h] = dot3(gap_hi[:, :mortar], gap_lo[:, :mortar], y_ref[p, h, 2 * face :, :])

    def face_end(p, h):
        chosen = pick(own_row, partner, cpart[p, h])
        for k in others:
            remote(cin.at[p, h, k - 1], cin.at[p, h, k - 1], cx_send.at[p, h, k - 1], cx_recv.at[p, h, k - 1],
                   near(other(k))).wait_recv()
            chosen = chosen + cin[p, h, k - 1]
        gap = own_gap[p, h] + dot3(gap_hi[:, mortar:], gap_lo[:, mortar:], chosen)
        pull_glue_end(p, h)
        return (y_ref[p, h, face : 2 * face, :] - gl[p, h]) * mask, gap

    def apply(w_value, p, h, first, plus):
        high, low = split(w_value)
        both = jnp.concatenate([high, low], axis=1)
        cut = pl.ds(first, w_value.shape[0])
        for i in (2, 0, 1):
            at = pl.ds(i * face, face)
            out = bdot(k_hi[at, cut], both)
            out = out[:, :half] + (out[:, half:] + bdot(k_lo[at, cut], high))
            if plus:
                out = out + base[h, at, :]
            y_ref[p, h, at, :] = out
            if i == 2:
                face_swap(p, h)
            if i == 0:
                pull_glue(p, h)

    def sums_start(n, h, values):
        padded = values + [jnp.zeros_like(values[0])] * (8 - len(values))
        r1[n, h, c] = jnp.concatenate(padded, axis=0)
        for k in range(1, n_group):
            begin(remote(r1.at[n, h, c], r1.at[n, h, c], r1_send.at[n, h, k], r1_recv.at[n, h, k],
                         near(lax.rem(c + k, n_group))))

    def sums_mid(n, h):
        for k in range(1, n_group):
            there = lax.rem(c - k + n_group, n_group)
            remote(r1.at[n, h, there], r1.at[n, h, there], r1_send.at[n, h, k], r1_recv.at[n, h, k], near(there)).wait_recv()
        r2[n, h, b] = jnp.sum(r1[n, h], axis=0)
        for k in range(1, n_bulk):
            begin(remote(r2.at[n, h, b], r2.at[n, h, b], r2_send.at[n, h, k], r2_recv.at[n, h, k],
                         {"bulk": lax.rem(b + k, n_bulk), "contact": c}))

    def sums_end(n, h):
        for k in range(1, n_bulk):
            there = lax.rem(b - k + n_bulk, n_bulk)
            remote(r2.at[n, h, there], r2.at[n, h, there], r2_send.at[n, h, k], r2_recv.at[n, h, k],
                   {"bulk": there, "contact": c}).wait_recv()
        return jnp.sum(r2[n, h], axis=0)

    def inner(*terms):
        return sum(jnp.sum(x * y, axis=0, keepdims=True) for x, y in terms)

    load_surface.wait()
    load_mm.wait()
    surface = surface_ref[0].astype(F32)
    mask = jnp.where(has_right, 1.0, 0.0).astype(F32)
    master = mm_ref[...] * surface
    high, low = split(master.T)
    adj_hi[mortar:, :] = high
    adj_lo[mortar:, :] = low
    load_lamc.wait()
    for h in range(2):
        tsrc[0, h] = adjoint(split(lamc_ref[:, cols(h)]), mortar)
    load_master.wait()
    own_master = jnp.full((8, half), master_ref[0].astype(F32), F32)
    own_row = own_master[0:1, :]
    meta_src[...] = own_master
    load_lamg.wait()

    pl.semaphore_wait(barrier, n_group - 1 + n_bulk - 1)
    begin(remote(meta_src, meta.at[0], m_send.at[0], m_recv.at[0], near(partner)))
    for h in range(2):
        mortar_swap(0, h)
    for k in others:
        begin(remote(meta_src, meta.at[k], m_send.at[k], m_recv.at[k], near(other(k))))
    for h in range(2):
        push_glue(lamg_ref.at[:, pl.ds(h * half, half)], 0, h)

    @pl.when(b == 0)
    def _():
        gp[...] = jnp.zeros_like(gp)

    @pl.when(b == n_bulk - 1)
    def _():
        gl[...] = jnp.zeros_like(gl)

    load_ms.wait()
    slave = ms_ref[...] * surface
    high, low = split(slave.T)
    adj_hi[:mortar, :] = high
    adj_lo[:mortar, :] = low
    remote(meta.at[0], meta.at[0], m_send.at[0], m_recv.at[0], near(partner)).wait_recv()
    for h in range(2):
        mortar_cross(0, h)
    for h in range(2):
        w_ref[0, h, 2 * face :, :] = adjoint(split(lamc_ref[:, cols(h)]), 0)
    for i, part in enumerate((slave, -master)):
        high, low = split(part)
        gap_hi[:, i * mortar : (i + 1) * mortar] = high
        gap_lo[:, i * mortar : (i + 1) * mortar] = low

    load_f.wait()
    high, low = split(-f_raw[...])
    f_hi[...] = high
    f_lo[...] = low

    @pl.loop(0, 3)
    def _(i):
        at = pl.ds(pl.multiple_of(i * face, face), face)
        k_load(i).wait()
        high, low = split(k_raw[at, :])
        k_hi[at, :] = high
        k_lo[at, :] = low
        out = bdot(k_hi[at, :], f_hi[...])
        out = out + (bdot(k_hi[at, :], f_lo[...]) + bdot(k_lo[at, :], f_hi[...]))
        for h in range(2):
            base[h, at, :] = out[:, h * half : (h + 1) * half]

    for k in others:
        remote(meta.at[k], meta.at[k], m_send.at[k], m_recv.at[k], near(partner)).wait_recv()
    load_kinds.wait()
    load_expand.wait()
    load_active.wait()

    for h in range(2):
        total = mortar_end(0, h)
        push_glue_end(0, h)
        own = w_ref[0, h, 2 * face :, :]
        w = jnp.concatenate([-gp[0, h], lamg_ref[:, cols(h)] * mask, own - total], axis=0)
        apply(w, 0, h, 0, True)
        face_cross(0, h)

    for h in range(2):
        grad_g, grad_c = face_end(0, h)
        kind = kinds_ref[0:1, cols(h)]
        length = expand_ref[0:1, cols(h)]
        expand = kind == 1
        chop = kind == 2
        held = active_ref[0, :, cols(h)].astype(F32)
        dir_c = jnp.where(chop, jnp.minimum(grad_c, 0.0) * held, grad_c * (1.0 - held)) * surface
        scale = jnp.where(expand, length, 1.0)
        z_c = scale * dir_c
        fix = jnp.where(expand, surface * jnp.maximum(z_c - lamc_ref[:, cols(h)], 0.0), 0.0)
        net = z_c - fix
        parts = split(net)
        tsrc[1, h] = adjoint(parts, mortar)
        mortar_swap(1, h)
        dir_g = jnp.where(chop, 0.0, grad_g)
        zg[0, h] = scale * dir_g
        push_glue(zg.at[0, h], 1, h)
        gg[h] = grad_g
        gc[h] = grad_c
        dg[h] = dir_g
        dc[h] = dir_c
        zc[0, h] = net
        w_ref[0, h, 2 * face :, :] = adjoint(parts, 0)
        parts = split(fix)
        tsrc[2, h] = adjoint(parts, mortar)
        mortar_swap(2, h)
        wfix[h] = adjoint(parts, 0)
        mortar_cross(1, h)

    for h in range(2):
        total = mortar_end(1, h)
        if h == 1:
            sums_mid(0, 0)
        push_glue_end(1, h)
        own = w_ref[0, h, 2 * face :, :]
        w = jnp.concatenate([-gp[1, h], zg[0, h], own - total], axis=0)
        w_ref[0, h] = w
        apply(w, 1, h, 0, False)
        sums_start(0, h, [
            inner((gg[h], dg[h]), (gc[h], dc[h])),
            inner((w, y_ref[1, h])),
        ])
        face_cross(1, h)

    for h in range(2):
        b_g, b_c = face_end(1, h)
        if h == 0:
            sums_mid(0, 1)
        imz_g[h] = b_g
        imz_c[h] = b_c
        sums = sums_end(0, h)
        step = jnp.where(kinds_ref[0:1, cols(h)] == 1, 1.0, sums[0:1] / sums[1:2])
        grad_c = gc[h] - step * b_c
        lam_c = lamc_ref[:, cols(h)] - step * zc[0, h]
        kind = kinds_ref[1:2, cols(h)]
        expand = kind == 1
        chop = kind == 2
        held = active_ref[1, :, cols(h)].astype(F32)
        scale = jnp.where(expand, expand_ref[0:1, cols(h)], 1.0)
        v_c = jnp.where(chop, jnp.minimum(grad_c, 0.0) * held, scale * (grad_c * (1.0 - held))) * surface
        net = v_c - jnp.where(expand, surface * jnp.maximum(v_c - lam_c, 0.0), 0.0)
        parts = split(net)
        tsrc[3, h] = adjoint(parts, mortar)
        mortar_swap(3, h)
        grad_g = gg[h] - step * b_g
        zg[1, h] = jnp.where(chop, 0.0, scale * grad_g)
        push_glue(zg.at[1, h], 2, h)
        zc[1, h] = net
        gg[h] = grad_g
        gc[h] = grad_c
        outg_ref[:, cols(h)] = lamg_ref[:, cols(h)] * mask - step * zg[0, h]
        outc_ref[:, cols(h)] = lam_c
        w_ref[1, h, 2 * face :, :] = adjoint(parts, 0)
        mortar_cross(3, h)
        mortar_cross(2, h)

    def scale_of(h):
        return jnp.where(kinds_ref[0:1, cols(h)] == 1, expand_ref[0:1, cols(h)], 1.0)

    for h in range(2):
        total = mortar_end(3, h)
        push_glue_end(2, h)
        own = w_ref[1, h, 2 * face :, :]
        w = jnp.concatenate([-gp[2, h], zg[1, h], own - total], axis=0)
        w_ref[1, h] = w
        apply(w, 3, h, 0, False)
        face_cross(3, h)
        w_f = wfix[h] - mortar_end(2, h)
        if h == 1:
            sums_mid(1, 0)
        apply(w_f, 2, h, 2 * face, False)
        w = w_ref[1, h]
        w_0 = jnp.concatenate([w_ref[0, h, : 2 * face, :], w_ref[0, h, 2 * face :, :] + w_f], axis=0)
        y_0 = y_ref[1, h] + y_ref[2, h]
        inverse = 1.0 / scale_of(h)
        y_v = y_ref[3, h]
        sums_start(1, h, [
            inner((w, y_0)) * inverse,
            inner((w, y_v)),
            inner((w_0, y_v)) * inverse,
            inner((gg[h], zg[1, h]), (gc[h], zc[1, h])),
            inner((gg[h], dg[h]), (gc[h], dc[h])),
            inner((w_0, y_0)) * inverse * inverse,
        ])
        face_cross(2, h)

    for h in range(2):
        b_g, b_c = face_end(3, h)
        f_g, f_c = face_end(2, h)
        if h == 0:
            sums_mid(1, 1)
        sums = sums_end(1, h)
        inverse = 1.0 / scale_of(h)
        kind = kinds_ref[1:2, cols(h)]
        gamma = jnp.where(kind == 0, sums[0:1] / sums[5:6], 0.0)
        curvature = sums[1:2] - gamma * (sums[2:3] + sums[0:1]) + gamma * gamma * sums[5:6]
        descent = sums[3:4] - gamma * sums[4:5]
        step = jnp.where(kind == 1, 1.0, descent / curvature)
        outg_ref[:, cols(h)] = outg_ref[:, cols(h)] - step * (zg[1, h] - gamma * dg[h])
        outc_ref[:, cols(h)] = outc_ref[:, cols(h)] - step * (zc[1, h] - gamma * dc[h])
        outgg_ref[:, cols(h)] = gg[h] - step * (b_g - gamma * ((imz_g[h] + f_g) * inverse))
        outgc_ref[:, cols(h)] = gc[h] - step * (b_c - gamma * ((imz_c[h] + f_c) * inverse))

    for copy in pending:
        copy.wait_send()
    for there, copy in late:
        @pl.when(there)
        def _(copy=copy):
            copy.wait_send()


def finish(a, b, c, d, oa, ob, oc, od, sem):
    copies = [pltpu.make_async_copy(x, y, sem.at[i]) for i, (x, y) in enumerate(((a, oa), (b, ob), (c, oc), (d, od)))]
    for copy in copies:
        copy.start()
    for copy in copies:
        copy.wait()


def settle(parts):
    shape = jax.ShapeDtypeStruct(parts[0].shape, F32)
    return tuple(pl.pallas_call(
        finish,
        out_shape=[shape] * 4,
        in_specs=[pl.BlockSpec(memory_space=pltpu.VMEM)] * 4,
        out_specs=[pl.BlockSpec(memory_space=pl.ANY)] * 4,
        scratch_shapes=[pltpu.SemaphoreType.DMA((4,))],
    )(*[pltpu.with_memory_space_constraint(x, pltpu.VMEM) for x in parts]))


def solution(mesh):
    n_bulk, n_group = mesh.shape["bulk"], mesh.shape["contact"]
    split_rows = P(("bulk", "contact"), None)
    ids = P(("bulk", "contact"))
    placed = (split_rows,) * 6 + (ids, ids, P(), P(None, ("bulk", "contact"), None), P())

    def per_device(k_inv, ms, mm, force, lam_g, lam_c, master_map, on_surface, kinds, active, expand_len):
        face, columns = lam_g.shape
        mortar = lam_c.shape[0]
        order = k_inv.shape[1]
        rows = 2 * face + mortar
        half = columns // 2
        cross = n_group // 2 - 1
        vmem = pltpu.VMEM
        dma = pltpu.SemaphoreType.DMA
        in_vmem = pl.BlockSpec(memory_space=vmem)
        anywhere = pl.BlockSpec(memory_space=pl.ANY)
        dual = lambda *lead: vmem(lead + (2, face, half), F32)
        lanes = lambda lead, *rest: vmem((lead, 2) + rest + (mortar, half), F32)
        pair_sems = lambda *dims: [dma(dims), dma(dims)]
        expand_len = expand_len.reshape(1, -1)
        return settle(pl.pallas_call(
            functools.partial(kernel, n_bulk, n_group),
            out_shape=[vmem((face, columns), F32)] * 4,
            in_specs=[anywhere] * 11,
            out_specs=[in_vmem] * 4,
            scratch_shapes=[
                pltpu.SMEM(master_map.shape, jnp.int32), pltpu.SMEM(on_surface.shape, jnp.int32),
                vmem(ms.shape, F32), vmem(mm.shape, F32), vmem(lam_g.shape, F32), vmem(lam_c.shape, F32),
                vmem(kinds.shape, jnp.int32), vmem(active.shape, jnp.int32), vmem(expand_len.shape, F32),
                vmem((rows, order), F32), vmem((rows, order), BF16), vmem((rows, order), BF16),
                vmem((order, columns), F32), vmem((order, columns), BF16), vmem((order, columns), BF16),
                vmem((2, rows, half), F32),
                vmem((mortar, 2 * mortar), BF16), vmem((mortar, 2 * mortar), BF16),
                vmem((2 * mortar, mortar), BF16), vmem((2 * mortar, mortar), BF16),
                vmem((2, 2, rows, half), F32), dual(), vmem((4, 2, rows, half), F32),
                dual(3), dual(4), dual(2), dual(2),
                lanes(4), lanes(4), lanes(4, cross), lanes(4, cross), lanes(4), lanes(4, cross), lanes(4, cross),
                dual(), dual(), dual(), dual(), dual(), dual(), dual(4),
                vmem((8, half), F32), vmem((n_group // 2, 8, half), F32),
                vmem((2, 2, n_group, 8, half), F32), vmem((2, 2, n_bulk, 8, half), F32),
                dma((10,)), dma((3,)), *pair_sems(3, 2), *pair_sems(4, 2),
                *pair_sems(4, 2), *pair_sems(4, 2, cross), *pair_sems(4, 2), *pair_sems(4, 2, cross),
                *pair_sems(n_group // 2), *pair_sems(2, 2, n_group), *pair_sems(2, 2, n_bulk),
            ],
            compiler_params=pltpu.CompilerParams(
                collective_id=0, has_side_effects=True, vmem_limit_bytes=60 * 1024 * 1024
            ),
        )(master_map, on_surface, k_inv, ms, mm, force, lam_g, lam_c, kinds, active, expand_len))

    return jax.shard_map(
        per_device, mesh=mesh, in_specs=placed, out_specs=(split_rows,) * 4, check_vma=False
    )
```

```python
import functools

import jax
import jax.numpy as jnp
from jax import lax
from jax.experimental import pallas as pl
from jax.experimental.pallas import tpu as pltpu
from jax.sharding import PartitionSpec as P

MESH = pl.DeviceIdType.MESH
F32 = jnp.float32
BF16 = jnp.bfloat16


def split(x):
    high = x.astype(BF16)
    return high, (x - high.astype(F32)).astype(BF16)


def bdot(a, b):
    return jnp.dot(a, b, preferred_element_type=F32)


def dot3(a_high, a_low, x):
    width = x.shape[1]
    high, low = split(x)
    both = bdot(a_high, jnp.concatenate([high, low], axis=1))
    return both[:, :width] + (both[:, width:] + bdot(a_low, high))


def kernel(
    n_bulk, n_group,
    master_hbm, surface_hbm, kinv_hbm, ms_hbm, mm_hbm, force_hbm, lamg_hbm, lamc_hbm, kinds_hbm, active_hbm, expand_hbm,
    outg_ref, outc_ref, outgg_ref, outgc_ref,
    master_ref, surface_ref, ms_ref, mm_ref, lamg_ref, lamc_ref, kinds_ref, active_ref, expand_ref,
    k_raw, k_hi, k_lo, f_raw, f_hi, f_lo, base, gap_hi, gap_lo, adj_hi, adj_lo,
    w_ref, wfix, y_ref, gp, gl, zg, zc, tsrc, tpart, tout, tin, cpart, cout, cin,
    dg, dc, gg, gc, imz_g, imz_c, own_gap, meta_src, meta, r1, r2,
    load_sem, k_sem, gp_send, gp_recv, gl_send, gl_recv, tp_send, tp_recv, tx_send, tx_recv,
    cp_send, cp_recv, cx_send, cx_recv, m_send, m_recv, r1_send, r1_recv, r2_send, r2_recv,
):
    face, columns = lamg_ref.shape
    mortar = lamc_ref.shape[0]
    rows = 2 * face + mortar
    half = columns // 2
    b = lax.axis_index("bulk")
    c = lax.axis_index("contact")
    pairs = n_group // 2
    q = lax.div(c, 2)
    r = lax.rem(c, 2)
    partner = 2 * q + 1 - r
    pending = []

    barrier = pltpu.get_barrier_semaphore()
    for k in range(1, n_group):
        pl.semaphore_signal(barrier, inc=1, device_id={"bulk": b, "contact": lax.rem(c + k, n_group)}, device_id_type=MESH)
    for k in range(1, n_bulk):
        pl.semaphore_signal(barrier, inc=1, device_id={"bulk": lax.rem(b + k, n_bulk), "contact": c}, device_id_type=MESH)

    def load(i, src, dst):
        copy = pltpu.make_async_copy(src, dst, load_sem.at[i])
        copy.start()
        return copy

    def k_load(i):
        at = pl.ds(pl.multiple_of(i * face, face), face)
        return pltpu.make_async_copy(kinv_hbm.at[at], k_raw.at[at], k_sem.at[i])

    load_mm = load(0, mm_hbm, mm_ref)
    load_lamc = load(1, lamc_hbm, lamc_ref)
    load_master = load(2, master_hbm, master_ref)
    load_surface = load(3, surface_hbm, surface_ref)
    load_lamg = load(4, lamg_hbm, lamg_ref)
    load_ms = load(5, ms_hbm, ms_ref)

    others = range(1, pairs)

    def other(k):
        return 2 * lax.rem(q + k, pairs) + r

    def remote(src, dst, send, recv, where):
        return pltpu.make_async_remote_copy(
            src_ref=src, dst_ref=dst, send_sem=send, recv_sem=recv, device_id=where, device_id_type=MESH
        )

    def begin(copy):
        copy.start()
        pending.append(copy)

    def near(where):
        return {"bulk": b, "contact": where}

    right = {"bulk": lax.rem(b + 1, n_bulk), "contact": c}
    left = {"bulk": lax.rem(b + n_bulk - 1, n_bulk), "contact": c}
    has_right = b < n_bulk - 1
    has_left = b > 0
    late = []

    def push_glue(src, p, h):
        copy = remote(src, gp.at[p, h], gp_send.at[p, h], gp_recv.at[p, h], right)

        @pl.when(has_right)
        def _():
            copy.start()

        late.append((has_right, copy))

    def push_glue_end(p, h):
        @pl.when(has_left)
        def _():
            remote(gp.at[p, h], gp.at[p, h], gp_send.at[p, h], gp_recv.at[p, h], left).wait_recv()

    def pull_glue(p, h):
        copy = remote(y_ref.at[p, h, pl.ds(0, face)], gl.at[p, h], gl_send.at[p, h], gl_recv.at[p, h], left)

        @pl.when(has_left)
        def _():
            copy.start()

        late.append((has_left, copy))

    def pull_glue_end(p, h):
        @pl.when(has_right)
        def _():
            remote(gl.at[p, h], gl.at[p, h], gl_send.at[p, h], gl_recv.at[p, h], right).wait_recv()

    def cols(h):
        return slice(h * half, (h + 1) * half)

    def pick(row, ident, value):
        return jnp.where(row == ident.astype(F32), value, 0.0)

    def adjoint(parts, first):
        high, low = parts
        cut = pl.ds(first, mortar)
        both = bdot(adj_hi[cut, :], jnp.concatenate([high, low], axis=1))
        return both[:, :half] + (both[:, half:] + bdot(adj_lo[cut, :], high))

    def mortar_swap(p, h):
        begin(remote(tsrc.at[p, h], tpart.at[p, h], tp_send.at[p, h], tp_recv.at[p, h], near(partner)))

    def mortar_cross(p, h):
        remote(tpart.at[p, h], tpart.at[p, h], tp_send.at[p, h], tp_recv.at[p, h], near(partner)).wait_recv()
        for k in others:
            to = other(k)
            tout[p, h, k - 1] = pick(own_row, to, tsrc[p, h]) + pick(meta[0, 0:1, :], to, tpart[p, h])
            begin(remote(tout.at[p, h, k - 1], tin.at[p, h, k - 1], tx_send.at[p, h, k - 1], tx_recv.at[p, h, k - 1], near(to)))

    def mortar_end(p, h):
        total = pick(meta[0, 0:1, :], c, tpart[p, h])
        for k in others:
            remote(tin.at[p, h, k - 1], tin.at[p, h, k - 1], tx_send.at[p, h, k - 1], tx_recv.at[p, h, k - 1],
                   near(other(k))).wait_recv()
            total = total + tin[p, h, k - 1]
        return total

    def face_swap(p, h):
        begin(remote(y_ref.at[p, h, pl.ds(2 * face, mortar)], cpart.at[p, h], cp_send.at[p, h], cp_recv.at[p, h], near(partner)))

    def face_cross(p, h):
        remote(cpart.at[p, h], cpart.at[p, h], cp_send.at[p, h], cp_recv.at[p, h], near(partner)).wait_recv()
        for k in others:
            row = meta[pairs - k, 0:1, :]
            cout[p, h, k - 1] = pick(row, c, y_ref[p, h, 2 * face :, :]) + pick(row, partner, cpart[p, h])
            begin(remote(cout.at[p, h, k - 1], cin.at[p, h, k - 1], cx_send.at[p, h, k - 1], cx_recv.at[p, h, k - 1],
                         near(other(k))))
        own_gap[p, h] = dot3(gap_hi[:, :mortar], gap_lo[:, :mortar], y_ref[p, h, 2 * face :, :])

    def face_end(p, h):
        chosen = pick(own_row, partner, cpart[p, h])
        for k in others:
            remote(cin.at[p, h, k - 1], cin.at[p, h, k - 1], cx_send.at[p, h, k - 1], cx_recv.at[p, h, k - 1],
                   near(other(k))).wait_recv()
            chosen = chosen + cin[p, h, k - 1]
        gap = own_gap[p, h] + dot3(gap_hi[:, mortar:], gap_lo[:, mortar:], chosen)
        pull_glue_end(p, h)
        return (y_ref[p, h, face : 2 * face, :] - gl[p, h]) * mask, gap

    def apply(w_value, p, h, first, plus, send=True, between=None):
        high, low = split(w_value)
        both = jnp.concatenate([high, low], axis=1)
        cut = pl.ds(first, w_value.shape[0])
        for i in (2, 0, 1):
            at = pl.ds(i * face, face)
            out = bdot(k_hi[at, cut], both)
            out = out[:, :half] + (out[:, half:] + bdot(k_lo[at, cut], high))
            if plus:
                out = out + base[h, at, :]
            y_ref[p, h, at, :] = out
            if send and i == 2:
                face_swap(p, h)
            if between is not None and i == 2:
                between()
            if send and i == 0:
                pull_glue(p, h)

    def sums_start(n, h, values):
        padded = values + [jnp.zeros_like(values[0])] * (8 - len(values))
        r1[n, h, c] = jnp.concatenate(padded, axis=0)
        for k in range(1, n_group):
            begin(remote(r1.at[n, h, c], r1.at[n, h, c], r1_send.at[n, h, k], r1_recv.at[n, h, k],
                         near(lax.rem(c + k, n_group))))

    def sums_mid(n, h):
        for k in range(1, n_group):
            there = lax.rem(c - k + n_group, n_group)
            remote(r1.at[n, h, there], r1.at[n, h, there], r1_send.at[n, h, k], r1_recv.at[n, h, k], near(there)).wait_recv()
        r2[n, h, b] = jnp.sum(r1[n, h], axis=0)
        for k in range(1, n_bulk):
            begin(remote(r2.at[n, h, b], r2.at[n, h, b], r2_send.at[n, h, k], r2_recv.at[n, h, k],
                         {"bulk": lax.rem(b + k, n_bulk), "contact": c}))

    def sums_end(n, h):
        for k in range(1, n_bulk):
            there = lax.rem(b - k + n_bulk, n_bulk)
            remote(r2.at[n, h, there], r2.at[n, h, there], r2_send.at[n, h, k], r2_recv.at[n, h, k],
                   {"bulk": there, "contact": c}).wait_recv()
        return jnp.sum(r2[n, h], axis=0)

    def inner(*terms):
        return sum(jnp.sum(x * y, axis=0, keepdims=True) for x, y in terms)

    load_mm.wait()
    load_surface.wait()
    load_f = load(6, force_hbm, f_raw)
    for i in range(3):
        k_load(i).start()
    load_kinds = load(7, kinds_hbm, kinds_ref)
    load_expand = load(8, expand_hbm, expand_ref)
    load_active = load(9, active_hbm, active_ref)
    surface = surface_ref[0].astype(F32)
    mask = jnp.where(has_right, 1.0, 0.0).astype(F32)
    master = mm_ref[...] * surface
    high, low = split(master.T)
    adj_hi[mortar:, :] = high
    adj_lo[mortar:, :] = low
    load_lamc.wait()
    for h in range(2):
        tsrc[0, h] = adjoint(split(lamc_ref[:, cols(h)]), mortar)
    load_master.wait()
    own_master = jnp.full((8, half), master_ref[0].astype(F32), F32)
    own_row = own_master[0:1, :]
    meta_src[...] = own_master
    load_lamg.wait()

    pl.semaphore_wait(barrier, n_group - 1 + n_bulk - 1)
    begin(remote(meta_src, meta.at[0], m_send.at[0], m_recv.at[0], near(partner)))
    for h in range(2):
        mortar_swap(0, h)
    for k in others:
        begin(remote(meta_src, meta.at[k], m_send.at[k], m_recv.at[k], near(other(k))))
    for h in range(2):
        push_glue(lamg_ref.at[:, pl.ds(h * half, half)], 0, h)

    @pl.when(b == 0)
    def _():
        gp[...] = jnp.zeros_like(gp)

    @pl.when(b == n_bulk - 1)
    def _():
        gl[...] = jnp.zeros_like(gl)

    load_ms.wait()
    slave = ms_ref[...] * surface
    high, low = split(slave.T)
    adj_hi[:mortar, :] = high
    adj_lo[:mortar, :] = low
    remote(meta.at[0], meta.at[0], m_send.at[0], m_recv.at[0], near(partner)).wait_recv()
    for h in range(2):
        mortar_cross(0, h)
    for h in range(2):
        w_ref[0, h, 2 * face :, :] = adjoint(split(lamc_ref[:, cols(h)]), 0)
    for i, part in enumerate((slave, -master)):
        high, low = split(part)
        gap_hi[:, i * mortar : (i + 1) * mortar] = high
        gap_lo[:, i * mortar : (i + 1) * mortar] = low

    load_f.wait()
    high, low = split(-f_raw[...])
    f_hi[...] = high
    f_lo[...] = low

    @pl.loop(0, 3)
    def _(i):
        at = pl.ds(pl.multiple_of(i * face, face), face)
        k_load(i).wait()
        high, low = split(k_raw[at, :])
        k_hi[at, :] = high
        k_lo[at, :] = low
        out = bdot(k_hi[at, :], f_hi[...])
        out = out + (bdot(k_hi[at, :], f_lo[...]) + bdot(k_lo[at, :], f_hi[...]))
        for h in range(2):
            base[h, at, :] = out[:, h * half : (h + 1) * half]

    for k in others:
        remote(meta.at[k], meta.at[k], m_send.at[k], m_recv.at[k], near(partner)).wait_recv()
    load_kinds.wait()
    load_expand.wait()
    load_active.wait()

    for h in range(2):
        total = mortar_end(0, h)
        push_glue_end(0, h)
        own = w_ref[0, h, 2 * face :, :]
        w = jnp.concatenate([-gp[0, h], lamg_ref[:, cols(h)] * mask, own - total], axis=0)
        apply(w, 0, h, 0, True)
        face_cross(0, h)

    for h in range(2):
        grad_g, grad_c = face_end(0, h)
        kind = kinds_ref[0:1, cols(h)]
        length = expand_ref[0:1, cols(h)]
        expand = kind == 1
        chop = kind == 2
        held = active_ref[0, :, cols(h)].astype(F32)
        dir_c = jnp.where(chop, jnp.minimum(grad_c, 0.0) * held, grad_c * (1.0 - held)) * surface
        scale = jnp.where(expand, length, 1.0)
        z_c = scale * dir_c
        fix = jnp.where(expand, surface * jnp.maximum(z_c - lamc_ref[:, cols(h)], 0.0), 0.0)
        net = z_c - fix
        parts = split(net)
        tsrc[1, h] = adjoint(parts, mortar)
        mortar_swap(1, h)
        dir_g = jnp.where(chop, 0.0, grad_g)
        zg[0, h] = scale * dir_g
        push_glue(zg.at[0, h], 1, h)
        gg[h] = grad_g
        gc[h] = grad_c
        dg[h] = dir_g
        dc[h] = dir_c
        zc[0, h] = net
        w_ref[0, h, 2 * face :, :] = adjoint(parts, 0)
        parts = split(fix)
        tsrc[2, h] = adjoint(parts, mortar)
        mortar_swap(2, h)
        wfix[h] = adjoint(parts, 0)
        mortar_cross(1, h)

    for h in range(2):
        total = mortar_end(1, h)
        push_glue_end(1, h)
        own = w_ref[0, h, 2 * face :, :]
        w = jnp.concatenate([-gp[1, h], zg[0, h], own - total], axis=0)
        w_ref[0, h] = w
        apply(w, 1, h, 0, False, True, (lambda: sums_mid(0, 0)) if h == 1 else None)
        sums_start(0, h, [
            inner((gg[h], dg[h]), (gc[h], dc[h])),
            inner((w, y_ref[1, h])),
        ])
        face_cross(1, h)

    for h in range(2):
        b_g, b_c = face_end(1, h)
        if h == 1:
            mortar_cross(2, 0)
            imz_g[...] = b_g
            imz_c[...] = b_c
        sums = sums_end(0, h)
        step = jnp.where(kinds_ref[0:1, cols(h)] == 1, 1.0, sums[0:1] / sums[1:2])
        grad_c = gc[h] - step * b_c
        lam_c = lamc_ref[:, cols(h)] - step * zc[0, h]
        kind = kinds_ref[1:2, cols(h)]
        expand = kind == 1
        chop = kind == 2
        held = active_ref[1, :, cols(h)].astype(F32)
        scale = jnp.where(expand, expand_ref[0:1, cols(h)], 1.0)
        v_c = jnp.where(chop, jnp.minimum(grad_c, 0.0) * held, scale * (grad_c * (1.0 - held))) * surface
        net = v_c - jnp.where(expand, surface * jnp.maximum(v_c - lam_c, 0.0), 0.0)
        parts = split(net)
        tsrc[3, h] = adjoint(parts, mortar)
        mortar_swap(3, h)
        if h == 0:
            sums_mid(0, 1)
        grad_g = gg[h] - step * b_g
        zg[1, h] = jnp.where(chop, 0.0, scale * grad_g)
        push_glue(zg.at[1, h], 2, h)
        zc[1, h] = net
        gg[h] = grad_g
        gc[h] = grad_c
        outg_ref[:, cols(h)] = lamg_ref[:, cols(h)] * mask - step * zg[0, h]
        outc_ref[:, cols(h)] = lam_c
        w_ref[1, h, 2 * face :, :] = adjoint(parts, 0)
        mortar_cross(3, h)

    def scale_of(h):
        return jnp.where(kinds_ref[0:1, cols(h)] == 1, expand_ref[0:1, cols(h)], 1.0)

    def step_sums(h):
        w = w_ref[1, h]
        w_0 = jnp.concatenate([w_ref[0, h, : 2 * face, :], w_ref[0, h, 2 * face :, :] + wfix[h]], axis=0)
        y_0 = y_ref[1, h] + y_ref[2, h]
        inverse = 1.0 / scale_of(h)
        y_v = y_ref[3, h]
        sums_start(1, h, [
            inner((w, y_0)) * inverse,
            inner((w, y_v)),
            inner((w_0, y_v)) * inverse,
            inner((gg[h], zg[1, h]), (gc[h], zc[1, h])),
            inner((gg[h], dg[h]), (gc[h], dc[h])),
            inner((w_0, y_0)) * inverse * inverse,
        ])

    def step_end(h):
        sums = sums_end(1, h)
        kind = kinds_ref[1:2, cols(h)]
        gamma = jnp.where(kind == 0, sums[0:1] / sums[5:6], 0.0)
        curvature = sums[1:2] - gamma * (sums[2:3] + sums[0:1]) + gamma * gamma * sums[5:6]
        descent = sums[3:4] - gamma * sums[4:5]
        return gamma, jnp.where(kind == 1, 1.0, descent / curvature)

    def move(h, gamma, step):
        outg_ref[:, cols(h)] = outg_ref[:, cols(h)] - step * (zg[1, h] - gamma * dg[h])
        outc_ref[:, cols(h)] = outc_ref[:, cols(h)] - step * (zc[1, h] - gamma * dc[h])

    for h in range(2):
        total = mortar_end(3, h)
        push_glue_end(2, h)
        own = w_ref[1, h, 2 * face :, :]
        w = jnp.concatenate([-gp[2, h], zg[1, h], own - total], axis=0)
        w_ref[1, h] = w
        apply(w, 3, h, 0, False, h == 1, (lambda: sums_mid(1, 0)) if h == 1 else None)
        if h == 1:
            face_cross(3, h)
        w_f = wfix[h] - mortar_end(2, h)
        wfix[h] = w_f
        apply(w_f, 2, h, 2 * face, False, h == 1)
        step_sums(h)
        if h == 0:
            mortar_cross(2, 1)

    gamma_first, step_first = step_end(0)
    back = gamma_first / scale_of(0)
    for i in (2, 0, 1):
        at = pl.ds(i * face, face)
        y_ref[3, 0, at, :] = y_ref[3, 0, at, :] - back * (y_ref[1, 0, at, :] + y_ref[2, 0, at, :])
        if i == 2:
            face_swap(3, 0)
        if i == 0:
            pull_glue(3, 0)
    face_cross(2, 1)
    face_cross(3, 0)
    sums_mid(1, 1)
    move(0, gamma_first, step_first)

    b_g, b_c = face_end(3, 1)
    f_g, f_c = face_end(2, 1)
    gamma, step = step_end(1)
    back = gamma / scale_of(1)
    outgg_ref[:, cols(1)] = gg[1] - step * (b_g - back * (imz_g[...] + f_g))
    outgc_ref[:, cols(1)] = gc[1] - step * (b_c - back * (imz_c[...] + f_c))
    move(1, gamma, step)
    b_g, b_c = face_end(3, 0)
    outgg_ref[:, cols(0)] = gg[0] - step_first * b_g
    outgc_ref[:, cols(0)] = gc[0] - step_first * b_c

    for copy in pending:
        copy.wait_send()
    for there, copy in late:
        @pl.when(there)
        def _(copy=copy):
            copy.wait_send()


def finish(a, b, c, d, oa, ob, oc, od, sem):
    copies = [pltpu.make_async_copy(x, y, sem.at[i]) for i, (x, y) in enumerate(((a, oa), (b, ob), (c, oc), (d, od)))]
    for copy in copies:
        copy.start()
    for copy in copies:
        copy.wait()


def settle(parts):
    shape = jax.ShapeDtypeStruct(parts[0].shape, F32)
    return tuple(pl.pallas_call(
        finish,
        out_shape=[shape] * 4,
        in_specs=[pl.BlockSpec(memory_space=pltpu.VMEM)] * 4,
        out_specs=[pl.BlockSpec(memory_space=pl.ANY)] * 4,
        scratch_shapes=[pltpu.SemaphoreType.DMA((4,))],
    )(*[pltpu.with_memory_space_constraint(x, pltpu.VMEM) for x in parts]))


def solution(mesh):
    n_bulk, n_group = mesh.shape["bulk"], mesh.shape["contact"]
    split_rows = P(("bulk", "contact"), None)
    ids = P(("bulk", "contact"))
    placed = (split_rows,) * 6 + (ids, ids, P(), P(None, ("bulk", "contact"), None), P())

    def per_device(k_inv, ms, mm, force, lam_g, lam_c, master_map, on_surface, kinds, active, expand_len):
        face, columns = lam_g.shape
        mortar = lam_c.shape[0]
        order = k_inv.shape[1]
        rows = 2 * face + mortar
        half = columns // 2
        cross = n_group // 2 - 1
        vmem = pltpu.VMEM
        dma = pltpu.SemaphoreType.DMA
        in_vmem = pl.BlockSpec(memory_space=vmem)
        anywhere = pl.BlockSpec(memory_space=pl.ANY)
        dual = lambda *lead: vmem(lead + (2, face, half), F32)
        lanes = lambda lead, *rest: vmem((lead, 2) + rest + (mortar, half), F32)
        pair_sems = lambda *dims: [dma(dims), dma(dims)]
        expand_len = expand_len.reshape(1, -1)
        return settle(pl.pallas_call(
            functools.partial(kernel, n_bulk, n_group),
            out_shape=[vmem((face, columns), F32)] * 4,
            in_specs=[anywhere] * 11,
            out_specs=[in_vmem] * 4,
            scratch_shapes=[
                pltpu.SMEM(master_map.shape, jnp.int32), pltpu.SMEM(on_surface.shape, jnp.int32),
                vmem(ms.shape, F32), vmem(mm.shape, F32), vmem(lam_g.shape, F32), vmem(lam_c.shape, F32),
                vmem(kinds.shape, jnp.int32), vmem(active.shape, jnp.int32), vmem(expand_len.shape, F32),
                vmem((rows, order), F32), vmem((rows, order), BF16), vmem((rows, order), BF16),
                vmem((order, columns), F32), vmem((order, columns), BF16), vmem((order, columns), BF16),
                vmem((2, rows, half), F32),
                vmem((mortar, 2 * mortar), BF16), vmem((mortar, 2 * mortar), BF16),
                vmem((2 * mortar, mortar), BF16), vmem((2 * mortar, mortar), BF16),
                vmem((2, 2, rows, half), F32), dual(), vmem((4, 2, rows, half), F32),
                dual(3), dual(4), dual(2), dual(2),
                lanes(4), lanes(4), lanes(4, cross), lanes(4, cross), lanes(4), lanes(4, cross), lanes(4, cross),
                dual(), dual(), dual(), dual(), vmem((face, half), F32), vmem((mortar, half), F32), dual(4),
                vmem((8, half), F32), vmem((n_group // 2, 8, half), F32),
                vmem((2, 2, n_group, 8, half), F32), vmem((2, 2, n_bulk, 8, half), F32),
                dma((10,)), dma((3,)), *pair_sems(3, 2), *pair_sems(4, 2),
                *pair_sems(4, 2), *pair_sems(4, 2, cross), *pair_sems(4, 2), *pair_sems(4, 2, cross),
                *pair_sems(n_group // 2), *pair_sems(2, 2, n_group), *pair_sems(2, 2, n_bulk),
            ],
            compiler_params=pltpu.CompilerParams(
                collective_id=0, has_side_effects=True, vmem_limit_bytes=60 * 1024 * 1024
            ),
        )(master_map, on_surface, k_inv, ms, mm, force, lam_g, lam_c, kinds, active, expand_len))

    return jax.shard_map(
        per_device, mesh=mesh, in_specs=placed, out_specs=(split_rows,) * 4, check_vma=False
    )
```
